128 devices in a mesh: gz: 4 (over z), xy: 32 (over x, y, core).
Axes of the slice: x: 4, y: 4, z: 4, core: 2. Of those that a mesh axis runs over, the one named last changes fastest.
Arguments:
- source_inner: float32 [8, 2, 16, 16384], P('gz', None, None, 'xy'), may hold values from -6 to 6
- source_front: float32 [8, 2, 16, 4096], P('gz', None, None, 'xy'), may hold values from -6 to 6
- inner_inverse: bfloat16 [8, 32, 2, 512, 512], P('gz', 'xy'), may hold values from -0.1875 to 0.1875
- coupling: bfloat16 [8, 32, 2, 512, 256], P('gz', 'xy'), may hold values from -0.1875 to 0.1875
- schur_inverse: bfloat16 [8, 2, 4096, 4096], P('gz', None, None, 'xy'), may hold values from -0.046875 to 0.046875
- front_rows: int32 [8, 8192], P('gz', 'xy'), may hold values from 0 to 4095, as said below
- link: float32 [8, 4096], P('gz', 'xy'), may hold values from 0.5 to 1.5
- front_size: int32 [8], P('gz'), may hold values from 2048 to 4096, as said below
Outputs:
- inner_field: float32 [8, 2, 16, 16384], P('gz', None, None, 'xy')
- front_field: float32 [8, 2, 16, 4096], P('gz', None, None, 'xy')
The draws below stay inside these ranges and needn't reach their ends.
Inputs may be any that keep to these rules, and one draw needn't show every extreme that they name: `front_rows`: within one local front of one panel the 256 entries are distinct. `front_size`: some panel has exactly 4096 live unknowns and some exactly half of 4096.
All inputs are finite; a program needn't handle non-finite values.
Results may differ from the reference program's by a relative error of at most 0.0075.
Values may be sent and summed in bfloat16 or wider, within the bound.
A program may use at most 64 MiB of HBM per device.

```python
import math
import jax
import jax.numpy as jnp
from jax import lax

F = 4096
BND = 256
LOC = 512
RHS = 16
PANELS = 8
N_XY = 32


def draw_front_rows(key, part):
    subkeys = jax.random.split(key, PANELS * N_XY)

    def pick_rows(subkey):
        return jax.random.permutation(subkey, F)[:BND]
    chosen = jax.vmap(pick_rows)(subkeys)
    return chosen.reshape(PANELS, N_XY * BND).astype(jnp.int32)


def draw_front_size(key, part):
    size_key = jax.random.fold_in(key, 11)
    place_key = jax.random.fold_in(key, 12)
    front_sizes = F // 2 + jax.random.randint(size_key, (PANELS,), 0, F // 2 + 1)
    placing = jax.random.permutation(place_key, PANELS)
    front_sizes = front_sizes.at[placing[0]].set(F).at[placing[1]].set(F // 2)
    return front_sizes.astype(jnp.int32)


def steps_of(own_key, extent, pieces, smallest, largest):
    def one(dim, parts):
        heights = jax.random.uniform(jax.random.fold_in(jax.random.fold_in(own_key, 6), dim), (parts,), jnp.float32, smallest / len(pieces), largest / len(pieces))
        return jnp.repeat(jnp.exp(heights), extent[dim] // parts).reshape((-1,) + (1,) * (len(extent) - dim - 1))

    level = one(*pieces[0])
    for cut in pieces[1:]:
        level = level * one(*cut)
    return level


def gaussian(key, extent, width, reach, pieces=(), kind=jnp.bfloat16):
    level = steps_of(key, extent, pieces, -0.22, 0.18) if pieces else 1.0
    drawn = jax.random.normal(key, extent, jnp.float32) * width * level
    return jnp.minimum(jnp.maximum(drawn, -reach), reach).astype(kind)


def setup_inputs(seed: int = 0) -> dict:
    seeds = jax.random.split(jax.random.key(seed), 9)
    source_inner = gaussian(seeds[0], (PANELS, 2, RHS, N_XY * LOC), 1.0, 6.0, ((0, 4), (3, 32)), jnp.float32)
    source_front = gaussian(seeds[1], (PANELS, 2, RHS, F), 1.0, 6.0, ((0, 4), (3, 32)), jnp.float32)
    inner_inverse = gaussian(seeds[2], (PANELS, N_XY, 2, LOC, LOC), (2 * LOC) ** -0.5, 0.1875, ((0, 4), (1, 32)))
    coupling = gaussian(seeds[3], (PANELS, N_XY, 2, LOC, BND), (2 * LOC) ** -0.5, 0.1875, ((0, 4), (1, 32)))
    schur_inverse = gaussian(seeds[4], (PANELS, 2, F, F), (4 * F) ** -0.5, 0.046875, ((0, 4), (3, 32)))
    front_rows = draw_front_rows(jax.random.fold_in(seeds[8], 71), 0)
    link = jnp.clip(jnp.exp(math.log(1.5) - 1.0986123 * jax.random.uniform(seeds[6], (PANELS, F), jnp.float32) ** steps_of(seeds[6], (PANELS, F), ((0, 4), (1, 32)), -0.2, 0.2)), 0.5, 1.5)
    front_size = draw_front_size(jax.random.fold_in(seeds[8], 71), 0)
    return {"source_inner": source_inner, "source_front": source_front, "inner_inverse": inner_inverse, "coupling": coupling, "schur_inverse": schur_inverse, "front_rows": front_rows, "link": link, "front_size": front_size}


def complex_product(field, matrix):
    row_count = field.shape[1]
    flattened = field.astype(jnp.bfloat16).reshape(2 * row_count, field.shape[2])
    first_part = jnp.dot(flattened, matrix[0], preferred_element_type=jnp.float32)
    second = jnp.dot(flattened, matrix[1], preferred_element_type=jnp.float32)
    return jnp.stack([first_part[:row_count] - second[row_count:], second[:row_count] + first_part[row_count:]])


def complex_product_t(field, matrix):
    row_count = field.shape[1]
    flattened = field.astype(jnp.bfloat16).reshape(2 * row_count, field.shape[2])
    contract = (((1,), (1,)), ((), ()))
    first_part = lax.dot_general(flattened, matrix[0], contract, preferred_element_type=jnp.float32)
    second = lax.dot_general(flattened, matrix[1], contract, preferred_element_type=jnp.float32)
    return jnp.stack([first_part[:row_count] - second[row_count:], second[:row_count] + first_part[row_count:]])


def reference(source_inner, source_front, inner_inverse, coupling, schur_inverse, front_rows, link, front_size):
    all_rows = jnp.arange(F, dtype=jnp.int32)
    solved_all = []
    bases = []
    masks = []
    for panel_index in range(PANELS):
        blocks = source_inner[panel_index].reshape(2, RHS, N_XY, LOC).transpose(2, 0, 1, 3)
        solved = jax.vmap(complex_product)(blocks, inner_inverse[panel_index])
        pushed = jax.vmap(complex_product)(solved, coupling[panel_index])
        flat_push = pushed.transpose(1, 2, 0, 3).reshape(2, RHS, N_XY * BND)
        contrib = jnp.zeros((2, RHS, F), jnp.float32).at[:, :, front_rows[panel_index]].add(flat_push)
        solved_all.append(solved)
        bases.append(source_front[panel_index] - contrib)
        masks.append((all_rows < front_size[panel_index]).astype(jnp.float32))
    fronts = []
    incoming = jnp.zeros((2, RHS, F), jnp.float32)
    for panel_index in range(PANELS):
        rhs_front = masks[panel_index] * (bases[panel_index] + link[panel_index] * incoming)
        incoming = masks[panel_index] * complex_product(rhs_front, schur_inverse[panel_index])
        fronts.append(incoming)
    totals = [None] * PANELS
    incoming = jnp.zeros((2, RHS, F), jnp.float32)
    for panel_index in reversed(range(PANELS)):
        change = masks[panel_index] * complex_product(masks[panel_index] * incoming, schur_inverse[panel_index])
        totals[panel_index] = fronts[panel_index] + change
        incoming = link[panel_index] * totals[panel_index]
    inner_out = []
    for panel_index in range(PANELS):
        picked = jnp.take(totals[panel_index], front_rows[panel_index].reshape(N_XY, BND), axis=2)
        picked = picked.transpose(2, 0, 1, 3)
        lifted = jax.vmap(complex_product_t)(picked, coupling[panel_index])
        back_part = jax.vmap(complex_product)(lifted, inner_inverse[panel_index])
        inner = solved_all[panel_index] - back_part
        inner_out.append(inner.transpose(1, 2, 0, 3).reshape(2, RHS, N_XY * LOC))
    return jnp.stack(inner_out), jnp.stack(totals)
```

```python
import functools

import jax
import jax.numpy as jnp
from jax import lax
from jax.experimental import pallas as pl
from jax.experimental.pallas import tpu as pltpu
from jax.sharding import PartitionSpec as P

MESH = pl.DeviceIdType.MESH
F32 = jnp.float32
BF16 = jnp.bfloat16
NT = (((1,), (1,)), ((), ()))
LANES = 128

FWD0, FWD1, BWD1, BWD0, TOT1, TOT0 = range(6)


def dot(a, b):
    return jnp.dot(a, b, preferred_element_type=F32)


def combined(first, second):
    half = first.shape[0] // 2
    return jnp.concatenate([first[:half] - second[half:], second[:half] + first[half:]], axis=0)


def kernel(
    side,
    depth,
    inner_hbm,
    front_hbm,
    inverse_hbm,
    coupling_hbm,
    schur_hbm,
    rows_hbm,
    link_hbm,
    size_ref,
    inner_out,
    front_out,
    inner_v,
    front_v,
    inverse_v,
    coupling_v,
    schur_v,
    rows_v,
    link_v,
    onehot,
    parts,
    landed,
    gathered,
    passed,
    passing,
    solved_v,
    inner_res,
    front_res,
    base_v,
    load_sem,
    store_sem,
    send_sem,
    gather_sem,
    contrib_sem,
    pass_send_sem,
    pass_recv_sem,
):
    chips = side * side
    peers = 2 * chips
    me = lax.axis_index("xy")
    turn = lax.axis_index("gz")
    core = lax.rem(me, 2)
    chip = me // 2
    chip_x = chip // side
    chip_y = lax.rem(chip, side)

    def chip_at(dx, dy):
        return lax.rem(chip_x + dx, side) * side + lax.rem(chip_y + dy, side)

    def distance(d):
        return min(d, side - d)

    offsets = sorted(
        ((dx, dy) for dx in range(side) for dy in range(side)),
        key=lambda d: (distance(d[0]) + distance(d[1]), d),
    )
    near_chips = [chip_at(*d) for d in offsets]
    far_first = [
        2 * c + lax.rem(core + q, 2) for c in reversed(near_chips[1:]) for q in range(2)
    ] + [2 * chip + 1 - core]

    loads = []

    def load(src, dst):
        copy = pltpu.make_async_copy(src, dst, load_sem.at[len(loads)])
        copy.start()
        loads.append(copy)
        return copy

    rows_load = load(rows_hbm, rows_v)
    inner_load = load(inner_hbm, inner_v)
    local_loads = []
    for p in range(2):
        local_loads.append((load(inverse_hbm.at[p], inverse_v.at[p]), load(coupling_hbm.at[p], coupling_v.at[p])))
    front_load = load(front_hbm, front_v)
    link_load = load(link_hbm, link_v)
    schur_loads = [
        [load(schur_hbm.at[p, i], schur_v.at[p, :, pl.ds(i * LANES, LANES)]) for i in range(2)]
        for p in range(2)
    ]

    barrier = pltpu.get_barrier_semaphore()
    for peer in far_first:
        pl.semaphore_signal(barrier, inc=1, device_id={"xy": peer}, device_id_type=MESH)

    @pl.when(turn > 0)
    def _():
        pl.semaphore_signal(barrier, inc=1, device_id={"gz": turn - 1}, device_id_type=MESH)

    @pl.when(turn < depth - 1)
    def _():
        pl.semaphore_signal(barrier, inc=1, device_id={"gz": turn + 1}, device_id_type=MESH)

    def local_part(p):
        iota = lax.broadcasted_iota(jnp.int32, (2 * LANES, 2 * LANES), 0)
        wanted = rows_v[p : p + 1, :]
        for c in range(chips):
            onehot[p, pl.ds(c * 2 * LANES, 2 * LANES), :] = (
                iota + c * 2 * LANES == wanted
            ).astype(F32).astype(BF16)
        for copy in local_loads[p]:
            copy.wait()
        field = inner_v[p].reshape(-1, inner_v.shape[-1]).astype(BF16)
        solved = combined(dot(field, inverse_v[p, 0]), dot(field, inverse_v[p, 1]))
        solved_v[p] = solved
        rounded = solved.astype(BF16)
        pushed = combined(dot(rounded, coupling_v[p, 0]), dot(rounded, coupling_v[p, 1])).astype(BF16)
        for c in range(chips):
            spread = lax.dot_general(
                pushed, onehot[p, pl.ds(c * 2 * LANES, 2 * LANES), :], NT, preferred_element_type=F32
            ).astype(BF16)
            parts[p, 2 * c] = spread[:, :LANES]
            parts[p, 2 * c + 1] = spread[:, LANES:]
        landed[p, me] = parts[p, me]

    def send_parts(p):
        for peer in far_first:
            pltpu.make_async_remote_copy(
                src_ref=parts.at[p, peer],
                dst_ref=landed.at[p, me],
                send_sem=send_sem.at[p],
                recv_sem=contrib_sem.at[p],
                device_id={"xy": peer},
                device_id_type=MESH,
            ).start()

    def wait_bytes(ref, sem):
        pltpu.make_async_copy(ref, ref, sem).wait()

    rows_load.wait()
    inner_load.wait()
    local_part(0)
    pl.semaphore_wait(barrier, peers - 1 + jnp.minimum(turn, 1) + jnp.minimum(depth - 1 - turn, 1))
    send_parts(0)
    local_part(1)
    send_parts(1)

    front_load.wait()
    link_load.wait()
    for p in range(2):
        wait_bytes(landed.at[p, pl.ds(0, peers - 1)], contrib_sem.at[p])
        total = landed[p, 0].astype(F32)
        for i in range(1, peers):
            total = total + landed[p, i].astype(F32)
        base_v[p] = front_v[p].reshape(total.shape) - total
        for copy in schur_loads[p]:
            copy.wait()

    own = me * LANES + lax.broadcasted_iota(jnp.int32, (1, LANES), 1)
    masks = [jnp.where(own < size_ref[p], 1.0, 0.0).astype(F32) for p in range(2)]
    links = [link_v[p : p + 1, :] for p in range(2)]

    def share(g, block):
        gathered[g, me] = block.astype(BF16)
        for peer in far_first:
            pltpu.make_async_remote_copy(
                src_ref=gathered.at[g, me],
                dst_ref=gathered.at[g, me],
                send_sem=send_sem.at[2 + g],
                recv_sem=gather_sem.at[g, chip],
                device_id={"xy": peer},
                device_id_type=MESH,
            ).start()

    def product(g, matrix, waits=True):
        total = None
        for i, c in enumerate(near_chips):
            if waits:
                if i == 0:
                    wait_bytes(gathered.at[g, 0], gather_sem.at[g, c])
                else:
                    wait_bytes(gathered.at[g, pl.ds(0, 2)], gather_sem.at[g, c])
            block = jnp.concatenate([gathered[g, 2 * c], gathered[g, 2 * c + 1]], axis=1)
            rows = pl.ds(pl.multiple_of(c * 2 * LANES, 2 * LANES), 2 * LANES)
            term = dot(block, matrix[rows, :])
            total = term if total is None else total + term
        return total

    def schur(g, p, waits=True):
        out = product(g, schur_v.at[p], waits)
        return combined(out[:, :LANES], out[:, LANES:])

    def hand_on(i, to):
        return pltpu.make_async_remote_copy(
            src_ref=passing.at[i],
            dst_ref=passed.at[i],
            send_sem=pass_send_sem.at[i],
            recv_sem=pass_recv_sem.at[i],
            device_id={"gz": to},
            device_id_type=MESH,
        )

    @pl.when(turn == 0)
    def _():
        passed[0] = jnp.zeros_like(passed[0])

    @pl.when(turn == depth - 1)
    def _():
        for i in range(peers):
            gathered[BWD1, i] = jnp.zeros_like(gathered[BWD1, i])
        front_res[1] = schur(BWD1, 1, waits=False)

    @pl.when(turn > 0)
    def _():
        hand_on(0, turn - 1).wait_recv()

    share(FWD0, masks[0] * (base_v[0] + links[0] * passed[0]))
    front0 = masks[0] * schur(FWD0, 0)
    share(FWD1, masks[1] * (base_v[1] + links[1] * front0))
    front1 = masks[1] * schur(FWD1, 1)

    @pl.when(turn < depth - 1)
    def _():
        passing[0] = front1
        hand_on(0, turn + 1).start()

    @pl.when(turn < depth - 1)
    def _():
        hand_on(1, turn + 1).wait_recv()
        share(BWD1, masks[1] * passed[1])
        front_res[1] = schur(BWD1, 1)

    total1 = front1 + masks[1] * front_res[1]
    share(BWD0, masks[0] * (links[1] * total1))
    front_res[1] = total1
    total0 = front0 + masks[0] * schur(BWD0, 0)

    @pl.when(turn > 0)
    def _():
        passing[1] = links[0] * total0
        hand_on(1, turn - 1).start()

    share(TOT0, total0)
    share(TOT1, total1)
    front_res[0] = total0
    front_store = pltpu.make_async_copy(front_res, front_out, store_sem.at[0])
    front_store.start()

    stores = []
    for p, g in ((1, TOT1), (0, TOT0)):
        picked = product(g, onehot.at[p]).astype(BF16)
        first = lax.dot_general(picked, coupling_v[p, 0], NT, preferred_element_type=F32)
        second = lax.dot_general(picked, coupling_v[p, 1], NT, preferred_element_type=F32)
        lifted = combined(first, second).astype(BF16)
        inner_res[p] = solved_v[p] - combined(dot(lifted, inverse_v[p, 0]), dot(lifted, inverse_v[p, 1]))
        store = pltpu.make_async_copy(inner_res.at[p], inner_out.at[p], store_sem.at[1 + p])
        store.start()
        stores.append(store)

    for p in range(2):
        wait_bytes(parts.at[p, pl.ds(0, peers - 1)], send_sem.at[p])
    for g in (FWD0, FWD1, BWD0, TOT1, TOT0):
        wait_bytes(gathered.at[g, pl.ds(0, peers - 1)], send_sem.at[2 + g])

    @pl.when(turn < depth - 1)
    def _():
        wait_bytes(gathered.at[BWD1, pl.ds(0, peers - 1)], send_sem.at[2 + BWD1])
        hand_on(0, turn + 1).wait_send()

    @pl.when(turn > 0)
    def _():
        hand_on(1, turn - 1).wait_send()

    front_store.wait()
    for store in stores:
        store.wait()


def solution(mesh):
    n_xy = mesh.shape["xy"]
    depth = mesh.shape["gz"]
    side = round((n_xy // 2) ** 0.5)

    def on_device(inner, front, inverse, coupling, schur, rows, link, size):
        panels, two, rhs, loc = inner.shape
        both = two * rhs
        unknowns = schur.shape[2]
        bnd = coupling.shape[-1]
        inverse = inverse.reshape(panels, two, loc, loc)
        coupling = coupling.reshape(panels, two, loc, bnd)
        inner = inner.reshape(panels, both, loc)
        front = front.reshape(panels, both, LANES)
        hbm = pl.BlockSpec(memory_space=pltpu.HBM)
        vmem = pltpu.VMEM
        inner_out, front_out = pl.pallas_call(
            functools.partial(kernel, side, depth),
            out_shape=(
                jax.ShapeDtypeStruct(inner.shape, F32),
                jax.ShapeDtypeStruct(front.shape, F32),
            ),
            in_specs=[hbm] * 7 + [pl.BlockSpec(memory_space=pltpu.SMEM)],
            out_specs=(hbm, hbm),
            scratch_shapes=[
                vmem(inner.shape, F32),
                vmem(front.shape, F32),
                vmem(inverse.shape, BF16),
                vmem(coupling.shape, BF16),
                vmem((panels, unknowns, 2 * LANES), BF16),
                vmem(rows.shape, jnp.int32),
                vmem(link.shape, F32),
                vmem((panels, unknowns, bnd), BF16),
                vmem((panels, n_xy, both, LANES), BF16),
                vmem((panels, n_xy, both, LANES), BF16),
                vmem((6, n_xy, both, LANES), BF16),
                vmem((2, both, LANES), F32),
                vmem((2, both, LANES), F32),
                vmem(inner.shape, F32),
                vmem(inner.shape, F32),
                vmem(front.shape, F32),
                vmem(front.shape, F32),
                pltpu.SemaphoreType.DMA((12,)),
                pltpu.SemaphoreType.DMA((3,)),
                pltpu.SemaphoreType.DMA((8,)),
                pltpu.SemaphoreType.DMA((6, n_xy // 2)),
                pltpu.SemaphoreType.DMA((2,)),
                pltpu.SemaphoreType.DMA((2,)),
                pltpu.SemaphoreType.DMA((2,)),
            ],
            compiler_params=pltpu.CompilerParams(
                collective_id=0, has_side_effects=True, vmem_limit_bytes=60 << 20
            ),
            name="sweep",
        )(inner, front, inverse, coupling, schur, rows, link, size)
        return (
            inner_out.reshape(panels, two, rhs, loc),
            front_out.reshape(panels, two, rhs, LANES),
        )

    placed = (
        P("gz", None, None, "xy"),
        P("gz", None, None, "xy"),
        P("gz", "xy", None, None, None),
        P("gz", "xy", None, None, None),
        P("gz", None, None, "xy"),
        P("gz", "xy"),
        P("gz", "xy"),
        P("gz"),
    )
    return jax.shard_map(
        on_device,
        mesh=mesh,
        in_specs=placed,
        out_specs=(P("gz", None, None, "xy"), P("gz", None, None, "xy")),
        check_vma=False,
    )
```

```python
import functools

import jax
import jax.numpy as jnp
from jax import lax
from jax.experimental import pallas as pl
from jax.experimental.pallas import tpu as pltpu
from jax.sharding import PartitionSpec as P

MESH = pl.DeviceIdType.MESH
F32 = jnp.float32
BF16 = jnp.bfloat16
NT = (((1,), (1,)), ((), ()))
LANES = 128

ROWS = 16
HALVES = 2
FWD0, FWD1, BWD1, BWD0, TOT1, TOT0 = range(6)


def dot(a, b):
    return jnp.dot(a, b, preferred_element_type=F32)


def dot_t(a, b):
    return lax.dot_general(a, b, NT, preferred_element_type=F32)


def combined(first, second):
    pieces = []
    for start in range(0, first.shape[0], ROWS):
        mid, end = start + ROWS // 2, start + ROWS
        pieces += [first[start:mid] - second[mid:end], second[start:mid] + first[mid:end]]
    return jnp.concatenate(pieces, axis=0)


def kernel(
    side,
    depth,
    inner_hbm,
    front_hbm,
    inverse_hbm,
    coupling_hbm,
    schur_hbm,
    rows_hbm,
    link_hbm,
    size_ref,
    inner_out,
    front_out,
    inner_v,
    front_v,
    inverse_v,
    coupling_v,
    schur_v,
    rows_v,
    link_v,
    onehot,
    parts,
    landed,
    gathered,
    crossing,
    ahead,
    ahead_in,
    mask_out,
    mask_in,
    base_v,
    first_v,
    last_v,
    solved_v,
    inner_res,
    front_res,
    load_sem,
    store_sem,
    contrib_send,
    contrib_sem,
    gather_send,
    gather_sem,
    cross_send,
    near_send,
    near_sem,
    side_send,
    side_sem,
):
    chips = side * side
    peers = 2 * chips
    me = lax.axis_index("xy")
    turn = lax.axis_index("gz")
    core = lax.rem(me, 2)
    chip = me // 2
    chip_x = chip // side
    chip_y = lax.rem(chip, side)

    def chip_at(dx, dy):
        return lax.rem(chip_x + dx, side) * side + lax.rem(chip_y + dy, side)

    def distance(d):
        return min(d, side - d)

    offsets = sorted(
        ((dx, dy) for dx in range(side) for dy in range(side)),
        key=lambda d: (distance(d[0]) + distance(d[1]), d),
    )
    near_chips = [chip_at(*d) for d in offsets]
    far_first = [
        2 * c + lax.rem(core + q, 2) for c in reversed(near_chips[1:]) for q in range(2)
    ] + [2 * chip + 1 - core]

    loads = []

    def load(src, dst):
        copy = pltpu.make_async_copy(src, dst, load_sem.at[len(loads)])
        copy.start()
        loads.append(copy)
        return copy

    rows_load = load(rows_hbm, rows_v)
    inner_load = load(inner_hbm, inner_v)
    local_loads = []
    for p in range(2):
        local_loads.append((load(inverse_hbm.at[p], inverse_v.at[p]), load(coupling_hbm.at[p], coupling_v.at[p])))
    front_load = load(front_hbm, front_v)
    link_load = load(link_hbm, link_v)
    schur_loads = [
        [load(schur_hbm.at[p, i], schur_v.at[p, :, pl.ds(i * LANES, LANES)]) for i in range(2)]
        for p in range(2)
    ]

    barrier = pltpu.get_barrier_semaphore()

    def greet(where):
        pl.semaphore_signal(barrier, inc=1, device_id=where, device_id_type=MESH)

    for peer in far_first:
        greet({"xy": peer})

    @pl.when(turn > 0)
    def _():
        for peer in far_first + [me]:
            greet({"xy": peer, "gz": turn - 1})

    @pl.when(turn < depth - 1)
    def _():
        for peer in far_first + [me]:
            greet({"xy": peer, "gz": turn + 1})

    def wait_bytes(ref, sem):
        pltpu.make_async_copy(ref, ref, sem).wait()

    def halves_of(ref, p):
        return jnp.concatenate([ref[p, i, h] for h in range(HALVES) for i in range(2)], axis=0)

    def local_part(p):
        iota = lax.broadcasted_iota(jnp.int32, (2 * LANES, 2 * LANES), 0)
        wanted = rows_v[p : p + 1, :]
        for c in range(chips):
            onehot[p, pl.ds(c * 2 * LANES, 2 * LANES), :] = (
                iota + c * 2 * LANES == wanted
            ).astype(F32).astype(BF16)
        for copy in local_loads[p]:
            copy.wait()
        field = halves_of(inner_v, p).astype(BF16)
        solved = combined(dot(field, inverse_v[p, 0]), dot(field, inverse_v[p, 1]))
        solved_v[p] = solved
        rounded = solved.astype(BF16)
        pushed = combined(dot(rounded, coupling_v[p, 0]), dot(rounded, coupling_v[p, 1])).astype(BF16)
        for c in range(chips):
            spread = dot_t(pushed, onehot[p, pl.ds(c * 2 * LANES, 2 * LANES), :]).astype(BF16)
            for h in range(HALVES):
                for q in range(2):
                    parts[p, h, 2 * c + q] = spread[h * ROWS : (h + 1) * ROWS, q * LANES : (q + 1) * LANES]
        for h in range(HALVES):
            landed[p, h, me] = parts[p, h, me]

    def send_parts(p):
        for h in range(HALVES):
            for peer in far_first:
                pltpu.make_async_remote_copy(
                    src_ref=parts.at[p, h, peer],
                    dst_ref=landed.at[p, h, me],
                    send_sem=contrib_send.at[p, h],
                    recv_sem=contrib_sem.at[p, h],
                    device_id={"xy": peer},
                    device_id_type=MESH,
                ).start()

    rows_load.wait()
    inner_load.wait()
    local_part(0)
    pl.semaphore_wait(
        barrier, peers - 1 + peers * (jnp.minimum(turn, 1) + jnp.minimum(depth - 1 - turn, 1))
    )
    send_parts(0)
    local_part(1)
    send_parts(1)
    front_load.wait()
    link_load.wait()

    own = me * LANES + lax.broadcasted_iota(jnp.int32, (1, LANES), 1)
    masks = [jnp.where(own < size_ref[p], 1.0, 0.0).astype(F32) for p in range(2)]
    links = [link_v[p : p + 1, :] for p in range(2)]

    def to_next():
        return pltpu.make_async_remote_copy(
            src_ref=mask_out,
            dst_ref=mask_in,
            send_sem=side_send.at[0],
            recv_sem=side_sem.at[0],
            device_id={"gz": turn + 1},
            device_id_type=MESH,
        )

    def to_previous():
        return pltpu.make_async_remote_copy(
            src_ref=ahead,
            dst_ref=ahead_in,
            send_sem=side_send.at[1],
            recv_sem=side_sem.at[1],
            device_id={"gz": turn - 1},
            device_id_type=MESH,
        )

    @pl.when(turn < depth - 1)
    def _():
        mask_out[...] = jnp.broadcast_to(masks[1], mask_out.shape)
        to_next().start()

    def share(g, h, block):
        gathered[g, h, me] = block.astype(BF16)
        for peer in far_first:
            pltpu.make_async_remote_copy(
                src_ref=gathered.at[g, h, me],
                dst_ref=gathered.at[g, h, me],
                send_sem=gather_send.at[g, h],
                recv_sem=gather_sem.at[g, h, chip],
                device_id={"xy": peer},
                device_id_type=MESH,
            ).start()

    near = sum(sum(map(distance, d)) < 2 for d in offsets)
    cross_order = far_first[: 2 * (chips - near)] + [2 * c + core for c in reversed(near_chips[:near])]

    def cross(i, g, h, block, to):
        crossing[i, h] = block.astype(BF16)
        for peer in cross_order:
            pltpu.make_async_remote_copy(
                src_ref=crossing.at[i, h],
                dst_ref=gathered.at[g, h, me],
                send_sem=cross_send.at[i, h],
                recv_sem=gather_sem.at[g, h, chip],
                device_id={"xy": peer, "gz": to},
                device_id_type=MESH,
            ).start()

    def base_of(p, h):
        wait_bytes(landed.at[p, h, pl.ds(0, peers - 1)], contrib_sem.at[p, h])
        total = landed[p, h, 0].astype(F32)
        for i in range(1, peers):
            total = total + landed[p, h, i].astype(F32)
        return jnp.concatenate([front_v[p, i, h] for i in range(2)], axis=0) - total

    for h in range(HALVES):
        base = base_of(0, h)
        masked = masks[0] * base

        @pl.when(turn == 0)
        def _():
            share(FWD0, h, masks[0] * (base + links[0] * jnp.zeros_like(base)))

        @pl.when(turn > 0)
        def _():
            ahead[pl.ds(h * ROWS, ROWS), :] = masked

    @pl.when(turn > 0)
    def _():
        ahead[pl.ds(HALVES * ROWS, 8), :] = jnp.broadcast_to(masks[0] * links[0], (8, LANES))
        to_previous().start()

    for h in range(HALVES):
        base_v[h] = base_of(1, h)
    for p in range(2):
        for copy in schur_loads[p]:
            copy.wait()

    def product(g, h, matrix, arrival):
        total = None
        for i, c in enumerate(near_chips):
            if arrival is not None:
                arrival(g, h, i, c)
            block = jnp.concatenate([gathered[g, h, 2 * c], gathered[g, h, 2 * c + 1]], axis=1)
            rows = pl.ds(pl.multiple_of(c * 2 * LANES, 2 * LANES), 2 * LANES)
            term = dot(block, matrix[rows, :])
            total = term if total is None else total + term
        return total

    def shared(g, h, i, c):
        wait_bytes(gathered.at[g, h, pl.ds(0, 1 if i == 0 else 2)], gather_sem.at[g, h, c])

    def handed(i, g, h, j):
        slot = 2 * near_chips[j] + core
        return pltpu.make_async_remote_copy(
            src_ref=gathered.at[g, h, slot],
            dst_ref=gathered.at[g, h, slot],
            send_sem=near_send.at[i, h],
            recv_sem=near_sem.at[i, h, j],
            device_id={"xy": 2 * chip + 1 - core},
            device_id_type=MESH,
        )

    def hand_over(i, g, h):
        for j in range(near):
            wait_bytes(gathered.at[g, h, 0], gather_sem.at[g, h, near_chips[j]])
            handed(i, g, h, j).start()

    def crossed(i):
        def wait(g, h, j, c):
            if j < near:
                wait_bytes(gathered.at[g, h, 0], near_sem.at[i, h, j])
            else:
                wait_bytes(gathered.at[g, h, pl.ds(0, 2)], gather_sem.at[g, h, c])

        return wait

    def schur(g, h, p, arrival):
        out = product(g, h, schur_v.at[p], arrival)
        return combined(out[:, :LANES], out[:, LANES:])

    @pl.when(turn == depth - 1)
    def _():
        for h in range(HALVES):
            for i in range(peers):
                gathered[BWD1, h, i] = jnp.zeros((ROWS, LANES), BF16)
            last_v[h] = masks[1] * schur(BWD1, h, 1, None)

    for h in range(HALVES):

        @pl.when(turn == 0)
        def _():
            first_v[h] = masks[0] * schur(FWD0, h, 0, shared)

        @pl.when(turn > 0)
        def _():
            hand_over(0, FWD0, h)
            first_v[h] = masks[0] * schur(FWD0, h, 0, crossed(0))

        front = first_v[h]
        share(FWD1, h, masks[1] * (base_v[h] + links[1] * front))

    @pl.when(turn < depth - 1)
    def _():
        pltpu.make_async_copy(ahead_in, ahead_in, side_sem.at[1]).wait()

    for h in range(HALVES):
        front = masks[1] * schur(FWD1, h, 1, shared)

        @pl.when(turn < depth - 1)
        def _():
            cross(
                0,
                FWD0,
                h,
                ahead_in[pl.ds(h * ROWS, ROWS), :] + ahead_in[pl.ds(HALVES * ROWS, 1), :] * front,
                turn + 1,
            )
            last_v[h] = front

        @pl.when(turn == depth - 1)
        def _():
            total = front + last_v[h]
            share(BWD0, h, masks[0] * (links[1] * total))
            last_v[h] = total

    @pl.when(turn < depth - 1)
    def _():
        for h in range(HALVES):
            hand_over(1, BWD1, h)
            total = last_v[h] + masks[1] * schur(BWD1, h, 1, crossed(1))
            share(BWD0, h, masks[0] * (links[1] * total))
            last_v[h] = total

    @pl.when(turn == 0)
    def _():
        for h in range(HALVES):
            share(TOT1, h, last_v[h])

    @pl.when(turn > 0)
    def _():
        pltpu.make_async_copy(mask_in, mask_in, side_sem.at[0]).wait()

    for h in range(HALVES):
        total = first_v[h] + masks[0] * schur(BWD0, h, 0, shared)
        first_v[h] = total

        @pl.when(turn > 0)
        def _():
            cross(1, BWD1, h, mask_in[0:1, :] * (links[0] * total), turn - 1)

        @pl.when(turn == 0)
        def _():
            share(TOT0, h, total)

    @pl.when(turn > 0)
    def _():
        for h in range(HALVES):
            share(TOT0, h, first_v[h])
        for h in range(HALVES):
            share(TOT1, h, last_v[h])

    for h in range(HALVES):
        for i in range(2):
            rows = pl.ds(i * (ROWS // 2), ROWS // 2)
            front_res[0, i, h] = first_v[h, rows, :]
            front_res[1, i, h] = last_v[h, rows, :]
    stores = [pltpu.make_async_copy(front_res, front_out, store_sem.at[0])]
    stores[0].start()

    for p, g in ((1, TOT1), (0, TOT0)):
        for h in range(HALVES):
            picked = product(g, h, onehot.at[p], shared).astype(BF16)
            lifted = combined(dot_t(picked, coupling_v[p, 0]), dot_t(picked, coupling_v[p, 1])).astype(BF16)
            inner = solved_v[p, pl.ds(h * ROWS, ROWS), :] - combined(
                dot(lifted, inverse_v[p, 0]), dot(lifted, inverse_v[p, 1])
            )
            for i in range(2):
                inner_res[p, i, h] = inner[i * (ROWS // 2) : (i + 1) * (ROWS // 2)]
        store = pltpu.make_async_copy(inner_res.at[p], inner_out.at[p], store_sem.at[1 + p])
        store.start()
        stores.append(store)

    for h in range(HALVES):
        for p in range(2):
            wait_bytes(parts.at[p, h, pl.ds(0, peers - 1)], contrib_send.at[p, h])
        for g in (FWD1, BWD0, TOT1, TOT0):
            wait_bytes(gathered.at[g, h, pl.ds(0, peers - 1)], gather_send.at[g, h])

    @pl.when(turn == 0)
    def _():
        for h in range(HALVES):
            wait_bytes(gathered.at[FWD0, h, pl.ds(0, peers - 1)], gather_send.at[FWD0, h])

    @pl.when(turn < depth - 1)
    def _():
        for h in range(HALVES):
            wait_bytes(gathered.at[FWD0, h, pl.ds(0, len(cross_order))], cross_send.at[0, h])
            wait_bytes(gathered.at[BWD1, h, pl.ds(0, near)], near_send.at[1, h])
        to_next().wait_send()

    @pl.when(turn > 0)
    def _():
        for h in range(HALVES):
            wait_bytes(gathered.at[BWD1, h, pl.ds(0, len(cross_order))], cross_send.at[1, h])
            wait_bytes(gathered.at[FWD0, h, pl.ds(0, near)], near_send.at[0, h])
        to_previous().wait_send()

    for store in stores:
        store.wait()


def solution(mesh):
    n_xy = mesh.shape["xy"]
    depth = mesh.shape["gz"]
    side = round((n_xy // 2) ** 0.5)

    def on_device(inner, front, inverse, coupling, schur, rows, link, size):
        panels, two, rhs, loc = inner.shape
        unknowns = schur.shape[2]
        bnd = coupling.shape[-1]
        both = two * rhs
        inverse = inverse.reshape(panels, two, loc, loc)
        coupling = coupling.reshape(panels, two, loc, bnd)
        inner = inner.reshape(panels, two, HALVES, rhs // HALVES, loc)
        front = front.reshape(panels, two, HALVES, rhs // HALVES, LANES)
        hbm = pl.BlockSpec(memory_space=pltpu.HBM)
        vmem = pltpu.VMEM
        dma = pltpu.SemaphoreType.DMA
        inner_out, front_out = pl.pallas_call(
            functools.partial(kernel, side, depth),
            out_shape=(
                jax.ShapeDtypeStruct(inner.shape, F32),
                jax.ShapeDtypeStruct(front.shape, F32),
            ),
            in_specs=[hbm] * 7 + [pl.BlockSpec(memory_space=pltpu.SMEM)],
            out_specs=(hbm, hbm),
            scratch_shapes=[
                vmem(inner.shape, F32),
                vmem(front.shape, F32),
                vmem(inverse.shape, BF16),
                vmem(coupling.shape, BF16),
                vmem((panels, unknowns, 2 * LANES), BF16),
                vmem(rows.shape, jnp.int32),
                vmem(link.shape, F32),
                vmem((panels, unknowns, bnd), BF16),
                vmem((panels, HALVES, n_xy, ROWS, LANES), BF16),
                vmem((panels, HALVES, n_xy, ROWS, LANES), BF16),
                vmem((6, HALVES, n_xy, ROWS, LANES), BF16),
                vmem((2, HALVES, ROWS, LANES), BF16),
                vmem((HALVES * ROWS + 8, LANES), F32),
                vmem((HALVES * ROWS + 8, LANES), F32),
                vmem((8, LANES), F32),
                vmem((8, LANES), F32),
                vmem((HALVES, ROWS, LANES), F32),
                vmem((HALVES, ROWS, LANES), F32),
                vmem((HALVES, ROWS, LANES), F32),
                vmem((panels, both, loc), F32),
                vmem(inner.shape, F32),
                vmem(front.shape, F32),
                dma((12,)),
                dma((3,)),
                dma((2, HALVES)),
                dma((2, HALVES)),
                dma((6, HALVES)),
                dma((6, HALVES, n_xy // 2)),
                dma((2, HALVES)),
                dma((2, HALVES)),
                dma((2, HALVES, 5)),
                dma((2,)),
                dma((2,)),
            ],
            compiler_params=pltpu.CompilerParams(
                collective_id=0, has_side_effects=True, vmem_limit_bytes=60 << 20
            ),
            name="sweep",
        )(inner, front, inverse, coupling, schur, rows, link, size)
        return (
            inner_out.reshape(panels, two, rhs, loc),
            front_out.reshape(panels, two, rhs, LANES),
        )

    placed = (
        P("gz", None, None, "xy"),
        P("gz", None, None, "xy"),
        P("gz", "xy", None, None, None),
        P("gz", "xy", None, None, None),
        P("gz", None, None, "xy"),
        P("gz", "xy"),
        P("gz", "xy"),
        P("gz"),
    )
    return jax.shard_map(
        on_device,
        mesh=mesh,
        in_specs=placed,
        out_specs=(P("gz", None, None, "xy"), P("gz", None, None, "xy")),
        check_vma=False,
    )
```

```python
import functools

import jax
import jax.numpy as jnp
from jax import lax
from jax.experimental import pallas as pl
from jax.experimental.pallas import tpu as pltpu
from jax.sharding import PartitionSpec as P

MESH = pl.DeviceIdType.MESH
F32 = jnp.float32
BF16 = jnp.bfloat16
NT = (((1,), (1,)), ((), ()))
LANES = 128

ROWS = 16
HALVES = 2
FWD0, FWD1, BWD1, BWD0, TOT1, TOT0 = range(6)


def dot(a, b):
    return jnp.dot(a, b, preferred_element_type=F32)


def dot_t(a, b):
    return lax.dot_general(a, b, NT, preferred_element_type=F32)


def combined(first, second):
    pieces = []
    for start in range(0, first.shape[0], ROWS):
        mid, end = start + ROWS // 2, start + ROWS
        pieces += [first[start:mid] - second[mid:end], second[start:mid] + first[mid:end]]
    return jnp.concatenate(pieces, axis=0)


def kernel(
    side,
    depth,
    inner_hbm,
    front_hbm,
    inverse_hbm,
    coupling_hbm,
    schur_hbm,
    rows_hbm,
    link_hbm,
    size_hbm,
    inner_out,
    front_out,
    inner_v,
    front_v,
    inverse_v,
    coupling_v,
    schur_v,
    rows_v,
    link_v,
    size_ref,
    onehot,
    parts,
    landed,
    gathered,
    crossing,
    ahead,
    ahead_in,
    mask_out,
    mask_in,
    base_v,
    first_v,
    last_v,
    solved_v,
    inner_res,
    front_res,
    load_sem,
    store_sem,
    contrib_send,
    contrib_sem,
    gather_send,
    gather_sem,
    cross_send,
    near_send,
    near_sem,
    side_send,
    side_sem,
):
    chips = side * side
    peers = 2 * chips
    me = lax.axis_index("xy")
    turn = lax.axis_index("gz")
    core = lax.rem(me, 2)
    chip = me // 2
    chip_x = chip // side
    chip_y = lax.rem(chip, side)

    def chip_at(dx, dy):
        return lax.rem(chip_x + dx, side) * side + lax.rem(chip_y + dy, side)

    def distance(d):
        return min(d, side - d)

    offsets = sorted(
        ((dx, dy) for dx in range(side) for dy in range(side)),
        key=lambda d: (distance(d[0]) + distance(d[1]), d),
    )
    near_chips = [chip_at(*d) for d in offsets]
    far_first = [
        2 * c + lax.rem(core + q, 2) for c in reversed(near_chips[1:]) for q in range(2)
    ] + [2 * chip + 1 - core]

    loads = []

    def load(src, dst):
        copy = pltpu.make_async_copy(src, dst, load_sem.at[len(loads)])
        copy.start()
        loads.append(copy)
        return copy

    rows_load = load(rows_hbm, rows_v)
    inner_load = load(inner_hbm, inner_v)
    local_loads = []
    for p in range(2):
        local_loads.append((load(inverse_hbm.at[p], inverse_v.at[p]), load(coupling_hbm.at[p], coupling_v.at[p])))
    front_load = load(front_hbm, front_v)
    link_load = load(link_hbm, link_v)
    size_load = load(size_hbm, size_ref)
    schur_loads = [
        [load(schur_hbm.at[p, i], schur_v.at[p, :, pl.ds(i * LANES, LANES)]) for i in range(2)]
        for p in range(2)
    ]

    barrier = pltpu.get_barrier_semaphore()

    def greet(where):
        pl.semaphore_signal(barrier, inc=1, device_id=where, device_id_type=MESH)

    for peer in far_first:
        greet({"xy": peer})

    @pl.when(turn > 0)
    def _():
        greet({"gz": turn - 1})

    @pl.when(turn < depth - 1)
    def _():
        greet({"gz": turn + 1})

    def wait_bytes(ref, sem):
        pltpu.make_async_copy(ref, ref, sem).wait()

    def halves_of(ref, p):
        return jnp.concatenate([ref[p, i, h] for h in range(HALVES) for i in range(2)], axis=0)

    def local_part(p):
        iota = lax.broadcasted_iota(jnp.int32, (2 * LANES, 2 * LANES), 0)
        wanted = rows_v[p : p + 1, :]
        for c in range(chips):
            onehot[p, pl.ds(c * 2 * LANES, 2 * LANES), :] = (
                iota + c * 2 * LANES == wanted
            ).astype(F32).astype(BF16)
        for copy in local_loads[p]:
            copy.wait()
        field = halves_of(inner_v, p).astype(BF16)
        solved = combined(dot(field, inverse_v[p, 0]), dot(field, inverse_v[p, 1]))
        solved_v[p] = solved
        rounded = solved.astype(BF16)
        pushed = combined(dot(rounded, coupling_v[p, 0]), dot(rounded, coupling_v[p, 1])).astype(BF16)
        for c in range(chips):
            spread = dot_t(pushed, onehot[p, pl.ds(c * 2 * LANES, 2 * LANES), :]).astype(BF16)
            for h in range(HALVES):
                for q in range(2):
                    parts[p, h, 2 * c + q] = spread[h * ROWS : (h + 1) * ROWS, q * LANES : (q + 1) * LANES]
        for h in range(HALVES):
            landed[p, h, me] = parts[p, h, me]

    def send_parts(p):
        for h in range(HALVES):
            for peer in far_first:
                pltpu.make_async_remote_copy(
                    src_ref=parts.at[p, h, peer],
                    dst_ref=landed.at[p, h, me],
                    send_sem=contrib_send.at[p, h],
                    recv_sem=contrib_sem.at[p, h],
                    device_id={"xy": peer},
                    device_id_type=MESH,
                ).start()

    rows_load.wait()
    inner_load.wait()
    local_part(0)
    pl.semaphore_wait(
        barrier, peers - 1 + jnp.minimum(turn, 1) + jnp.minimum(depth - 1 - turn, 1)
    )
    send_parts(0)
    local_part(1)
    send_parts(1)
    front_load.wait()
    link_load.wait()
    size_load.wait()

    own = me * LANES + lax.broadcasted_iota(jnp.int32, (1, LANES), 1)
    masks = [jnp.where(own < size_ref[p], 1.0, 0.0).astype(F32) for p in range(2)]
    links = [link_v[p : p + 1, :] for p in range(2)]

    def to_next():
        return pltpu.make_async_remote_copy(
            src_ref=mask_out,
            dst_ref=mask_in,
            send_sem=side_send.at[0],
            recv_sem=side_sem.at[0],
            device_id={"gz": turn + 1},
            device_id_type=MESH,
        )

    def to_previous():
        return pltpu.make_async_remote_copy(
            src_ref=ahead,
            dst_ref=ahead_in,
            send_sem=side_send.at[1],
            recv_sem=side_sem.at[1],
            device_id={"gz": turn - 1},
            device_id_type=MESH,
        )

    @pl.when(turn < depth - 1)
    def _():
        mask_out[...] = jnp.broadcast_to(masks[1], mask_out.shape)
        to_next().start()

    def share(g, h, block):
        gathered[g, h, me] = block.astype(BF16)
        for peer in far_first:
            pltpu.make_async_remote_copy(
                src_ref=gathered.at[g, h, me],
                dst_ref=gathered.at[g, h, me],
                send_sem=gather_send.at[g, h],
                recv_sem=gather_sem.at[g, h, chip],
                device_id={"xy": peer},
                device_id_type=MESH,
            ).start()

    near = sum(sum(map(distance, d)) < 2 for d in offsets)
    cross_order = far_first[: 2 * (chips - near)] + [2 * c + core for c in reversed(near_chips[:near])]

    def cross(i, g, h, block, to):
        crossing[i, h] = block.astype(BF16)
        for peer in cross_order:
            pltpu.make_async_remote_copy(
                src_ref=crossing.at[i, h],
                dst_ref=gathered.at[g, h, me],
                send_sem=cross_send.at[i, h],
                recv_sem=gather_sem.at[g, h, chip],
                device_id={"xy": peer, "gz": to},
                device_id_type=MESH,
            ).start()

    def base_of(p, h):
        wait_bytes(landed.at[p, h, pl.ds(0, peers - 1)], contrib_sem.at[p, h])
        total = landed[p, h, 0].astype(F32)
        for i in range(1, peers):
            total = total + landed[p, h, i].astype(F32)
        return jnp.concatenate([front_v[p, i, h] for i in range(2)], axis=0) - total

    for h in range(HALVES):
        base = base_of(0, h)
        masked = masks[0] * base

        @pl.when(turn == 0)
        def _():
            share(FWD0, h, masks[0] * (base + links[0] * jnp.zeros_like(base)))

        @pl.when(turn > 0)
        def _():
            ahead[pl.ds(h * ROWS, ROWS), :] = masked

    @pl.when(turn > 0)
    def _():
        ahead[pl.ds(HALVES * ROWS, 8), :] = jnp.broadcast_to(masks[0] * links[0], (8, LANES))
        to_previous().start()

    for h in range(HALVES):
        base_v[h] = base_of(1, h)
    for p in range(2):
        for copy in schur_loads[p]:
            copy.wait()

    def product(g, h, matrix, arrival):
        total = None
        for i, c in enumerate(near_chips):
            if arrival is not None:
                arrival(g, h, i, c)
            block = jnp.concatenate([gathered[g, h, 2 * c], gathered[g, h, 2 * c + 1]], axis=1)
            rows = pl.ds(pl.multiple_of(c * 2 * LANES, 2 * LANES), 2 * LANES)
            term = dot(block, matrix[rows, :])
            total = term if total is None else total + term
        return total

    def shared(g, h, i, c):
        wait_bytes(gathered.at[g, h, pl.ds(0, 1 if i == 0 else 2)], gather_sem.at[g, h, c])

    def handed(i, g, h, j):
        slot = 2 * near_chips[j] + core
        return pltpu.make_async_remote_copy(
            src_ref=gathered.at[g, h, slot],
            dst_ref=gathered.at[g, h, slot],
            send_sem=near_send.at[i, h],
            recv_sem=near_sem.at[i, h, j],
            device_id={"xy": 2 * chip + 1 - core},
            device_id_type=MESH,
        )

    def hand_over(i, g, h):
        for j in range(near):
            wait_bytes(gathered.at[g, h, 0], gather_sem.at[g, h, near_chips[j]])
            handed(i, g, h, j).start()

    def crossed(i):
        def wait(g, h, j, c):
            if j < near:
                wait_bytes(gathered.at[g, h, 0], near_sem.at[i, h, j])
            else:
                wait_bytes(gathered.at[g, h, pl.ds(0, 2)], gather_sem.at[g, h, c])

        return wait

    def schur(g, h, p, arrival):
        out = product(g, h, schur_v.at[p], arrival)
        return combined(out[:, :LANES], out[:, LANES:])

    @pl.when(turn == depth - 1)
    def _():
        for h in range(HALVES):
            for i in range(peers):
                gathered[BWD1, h, i] = jnp.zeros((ROWS, LANES), BF16)
            last_v[h] = masks[1] * schur(BWD1, h, 1, None)

    for h in range(HALVES):

        @pl.when(turn == 0)
        def _():
            first_v[h] = masks[0] * schur(FWD0, h, 0, shared)

        @pl.when(turn > 0)
        def _():
            hand_over(0, FWD0, h)
            first_v[h] = masks[0] * schur(FWD0, h, 0, crossed(0))

        front = first_v[h]
        share(FWD1, h, masks[1] * (base_v[h] + links[1] * front))

    @pl.when(turn < depth - 1)
    def _():
        pltpu.make_async_copy(ahead_in, ahead_in, side_sem.at[1]).wait()

    for h in range(HALVES):
        front = masks[1] * schur(FWD1, h, 1, shared)

        @pl.when(turn < depth - 1)
        def _():
            cross(
                0,
                FWD0,
                h,
                ahead_in[pl.ds(h * ROWS, ROWS), :] + ahead_in[pl.ds(HALVES * ROWS, 1), :] * front,
                turn + 1,
            )
            last_v[h] = front

        @pl.when(turn == depth - 1)
        def _():
            total = front + last_v[h]
            share(BWD0, h, masks[0] * (links[1] * total))
            last_v[h] = total

    @pl.when(turn < depth - 1)
    def _():
        for h in range(HALVES):
            hand_over(1, BWD1, h)
            total = last_v[h] + masks[1] * schur(BWD1, h, 1, crossed(1))
            share(BWD0, h, masks[0] * (links[1] * total))
            last_v[h] = total

    @pl.when(turn == 0)
    def _():
        for h in range(HALVES):
            share(TOT1, h, last_v[h])

    @pl.when(turn > 0)
    def _():
        pltpu.make_async_copy(mask_in, mask_in, side_sem.at[0]).wait()

    for h in range(HALVES):
        total = first_v[h] + masks[0] * schur(BWD0, h, 0, shared)
        first_v[h] = total

        @pl.when(turn > 0)
        def _():
            cross(1, BWD1, h, mask_in[0:1, :] * (links[0] * total), turn - 1)

        @pl.when(turn == 0)
        def _():
            share(TOT0, h, total)

    @pl.when(turn > 0)
    def _():
        for h in range(HALVES):
            share(TOT0, h, first_v[h])
        for h in range(HALVES):
            share(TOT1, h, last_v[h])

    for h in range(HALVES):
        for i in range(2):
            rows = pl.ds(i * (ROWS // 2), ROWS // 2)
            front_res[0, i, h] = first_v[h, rows, :]
            front_res[1, i, h] = last_v[h, rows, :]

    stores = [pltpu.make_async_copy(front_res, front_out, store_sem.at[0])]
    stores[0].start()

    for p, g in ((1, TOT1), (0, TOT0)):
        for h in range(HALVES):
            picked = product(g, h, onehot.at[p], shared).astype(BF16)
            lifted = combined(dot_t(picked, coupling_v[p, 0]), dot_t(picked, coupling_v[p, 1])).astype(BF16)
            inner = solved_v[p, pl.ds(h * ROWS, ROWS), :] - combined(
                dot(lifted, inverse_v[p, 0]), dot(lifted, inverse_v[p, 1])
            )
            for i in range(2):
                inner_res[p, i, h] = inner[i * (ROWS // 2) : (i + 1) * (ROWS // 2)]

        store = pltpu.make_async_copy(inner_res.at[p], inner_out.at[p], store_sem.at[1 + p])
        store.start()
        stores.append(store)

    for h in range(HALVES):
        for p in range(2):
            wait_bytes(parts.at[p, h, pl.ds(0, peers - 1)], contrib_send.at[p, h])
        for g in (FWD1, BWD0, TOT1, TOT0):
            wait_bytes(gathered.at[g, h, pl.ds(0, peers - 1)], gather_send.at[g, h])

    @pl.when(turn == 0)
    def _():
        for h in range(HALVES):
            wait_bytes(gathered.at[FWD0, h, pl.ds(0, peers - 1)], gather_send.at[FWD0, h])

    @pl.when(turn < depth - 1)
    def _():
        for h in range(HALVES):
            wait_bytes(gathered.at[FWD0, h, pl.ds(0, len(cross_order))], cross_send.at[0, h])
            wait_bytes(gathered.at[BWD1, h, pl.ds(0, near)], near_send.at[1, h])
        to_next().wait_send()

    @pl.when(turn > 0)
    def _():
        for h in range(HALVES):
            wait_bytes(gathered.at[BWD1, h, pl.ds(0, len(cross_order))], cross_send.at[1, h])
            wait_bytes(gathered.at[FWD0, h, pl.ds(0, near)], near_send.at[0, h])
        to_previous().wait_send()

    for store in stores:
        store.wait()


def put(inner_in, front_in, inner_out, front_out, inner_v, front_v, sem):
    pairs = ((inner_in, inner_v, inner_out), (front_in, front_v, front_out))
    loads = [pltpu.make_async_copy(src, held, sem.at[0, i]) for i, (src, held, _) in enumerate(pairs)]
    stores = [pltpu.make_async_copy(held, dst, sem.at[1, i]) for i, (_, held, dst) in enumerate(pairs)]
    for copy in loads:
        copy.start()
    for copy, store in zip(loads, stores):
        copy.wait()
        store.start()
    for store in stores:
        store.wait()


def solution(mesh):
    n_xy = mesh.shape["xy"]
    depth = mesh.shape["gz"]
    side = round((n_xy // 2) ** 0.5)

    def on_device(inner, front, inverse, coupling, schur, rows, link, size):
        panels, two, rhs, loc = inner.shape
        unknowns = schur.shape[2]
        bnd = coupling.shape[-1]
        both = two * rhs
        inverse = inverse.reshape(panels, two, loc, loc)
        coupling = coupling.reshape(panels, two, loc, bnd)
        inner = inner.reshape(panels, two, HALVES, rhs // HALVES, loc)
        front = front.reshape(panels, two, HALVES, rhs // HALVES, LANES)
        hbm = pl.BlockSpec(memory_space=pltpu.HBM)
        vmem = pltpu.VMEM
        dma = pltpu.SemaphoreType.DMA
        inner_out, front_out = pl.pallas_call(
            functools.partial(kernel, side, depth),
            out_shape=(
                jax.ShapeDtypeStruct(inner.shape, F32),
                jax.ShapeDtypeStruct(front.shape, F32),
            ),
            in_specs=[hbm] * 8,
            out_specs=(hbm, hbm),
            scratch_shapes=[
                vmem(inner.shape, F32),
                vmem(front.shape, F32),
                vmem(inverse.shape, BF16),
                vmem(coupling.shape, BF16),
                vmem((panels, unknowns, 2 * LANES), BF16),
                vmem(rows.shape, jnp.int32),
                vmem(link.shape, F32),
                pltpu.SMEM(size.shape, jnp.int32),
                vmem((panels, unknowns, bnd), BF16),
                vmem((panels, HALVES, n_xy, ROWS, LANES), BF16),
                vmem((panels, HALVES, n_xy, ROWS, LANES), BF16),
                vmem((6, HALVES, n_xy, ROWS, LANES), BF16),
                vmem((2, HALVES, ROWS, LANES), BF16),
                vmem((HALVES * ROWS + 8, LANES), F32),
                vmem((HALVES * ROWS + 8, LANES), F32),
                vmem((8, LANES), F32),
                vmem((8, LANES), F32),
                vmem((HALVES, ROWS, LANES), F32),
                vmem((HALVES, ROWS, LANES), F32),
                vmem((HALVES, ROWS, LANES), F32),
                vmem((panels, both, loc), F32),
                vmem(inner.shape, F32),
                vmem(front.shape, F32),
                dma((13,)),
                dma((3,)),
                dma((2, HALVES)),
                dma((2, HALVES)),
                dma((6, HALVES)),
                dma((6, HALVES, n_xy // 2)),
                dma((2, HALVES)),
                dma((2, HALVES)),
                dma((2, HALVES, 5)),
                dma((2,)),
                dma((2,)),
            ],
            compiler_params=pltpu.CompilerParams(
                collective_id=0, has_side_effects=True, vmem_limit_bytes=60 << 20
            ),
            name="sweep",
        )(inner, front, inverse, coupling, schur, rows, link, size)
        inner_out, front_out = pl.pallas_call(
            put,
            out_shape=(
                jax.ShapeDtypeStruct(inner.shape, F32),
                jax.ShapeDtypeStruct(front.shape, F32),
            ),
            in_specs=[hbm, hbm],
            out_specs=(hbm, hbm),
            scratch_shapes=[vmem(inner.shape, F32), vmem(front.shape, F32), dma((2, 2))],
            compiler_params=pltpu.CompilerParams(vmem_limit_bytes=60 << 20),
            name="put",
        )(inner_out, front_out)
        return (
            inner_out.reshape(panels, two, rhs, loc),
            front_out.reshape(panels, two, rhs, LANES),
        )

    placed = (
        P("gz", None, None, "xy"),
        P("gz", None, None, "xy"),
        P("gz", "xy", None, None, None),
        P("gz", "xy", None, None, None),
        P("gz", None, None, "xy"),
        P("gz", "xy"),
        P("gz", "xy"),
        P("gz"),
    )
    return jax.shard_map(
        on_device,
        mesh=mesh,
        in_specs=placed,
        out_specs=(P("gz", None, None, "xy"), P("gz", None, None, "xy")),
        check_vma=False,
    )
```

```python
import functools

import jax
import jax.numpy as jnp
from jax import lax
from jax.experimental import pallas as pl
from jax.experimental.pallas import tpu as pltpu
from jax.sharding import PartitionSpec as P

MESH = pl.DeviceIdType.MESH
F32 = jnp.float32
BF16 = jnp.bfloat16
NT = (((1,), (1,)), ((), ()))
LANES = 128

ROWS = 16
HALVES = 2
FWD0, FWD1, BWD1, BWD0, TOT1, TOT0 = range(6)


def dot(a, b):
    return jnp.dot(a, b, preferred_element_type=F32)


def dot_t(a, b):
    return lax.dot_general(a, b, NT, preferred_element_type=F32)


def combined(first, second):
    pieces = []
    for start in range(0, first.shape[0], ROWS):
        mid, end = start + ROWS // 2, start + ROWS
        pieces += [first[start:mid] - second[mid:end], second[start:mid] + first[mid:end]]
    return jnp.concatenate(pieces, axis=0)


def kernel(
    side,
    depth,
    inner_hbm,
    front_hbm,
    inverse_hbm,
    coupling_hbm,
    schur_hbm,
    rows_hbm,
    link_hbm,
    size_hbm,
    inner_out,
    front_out,
    inner_v,
    front_v,
    inverse_v,
    coupling_v,
    schur_v,
    rows_v,
    link_v,
    size_ref,
    onehot,
    parts,
    landed,
    gathered,
    crossing,
    ahead,
    ahead_in,
    mask_out,
    mask_in,
    base_v,
    first_v,
    last_v,
    solved_v,
    inner_res,
    front_res,
    load_sem,
    store_sem,
    contrib_send,
    contrib_sem,
    gather_send,
    gather_sem,
    cross_send,
    near_send,
    near_sem,
    side_send,
    side_sem,
):
    chips = side * side
    peers = 2 * chips
    me = lax.axis_index("xy")
    turn = lax.axis_index("gz")
    core = lax.rem(me, 2)
    chip = me // 2
    chip_x = chip // side
    chip_y = lax.rem(chip, side)

    def chip_at(dx, dy):
        return lax.rem(chip_x + dx, side) * side + lax.rem(chip_y + dy, side)

    def distance(d):
        return min(d, side - d)

    offsets = sorted(
        ((dx, dy) for dx in range(side) for dy in range(side)),
        key=lambda d: (distance(d[0]) + distance(d[1]), d),
    )
    near_chips = [chip_at(*d) for d in offsets]
    far_first = [
        2 * c + lax.rem(core + q, 2) for c in reversed(near_chips[1:]) for q in range(2)
    ] + [2 * chip + 1 - core]

    loads = []

    def load(src, dst):
        copy = pltpu.make_async_copy(src, dst, load_sem.at[len(loads)])
        copy.start()
        loads.append(copy)
        return copy

    rows_load = load(rows_hbm, rows_v)
    inner_load = load(inner_hbm, inner_v)
    local_loads = []
    for p in range(2):
        local_loads.append((load(inverse_hbm.at[p], inverse_v.at[p]), load(coupling_hbm.at[p], coupling_v.at[p])))
    front_load = load(front_hbm, front_v)
    link_load = load(link_hbm, link_v)
    size_load = load(size_hbm, size_ref)
    schur_loads = [
        [load(schur_hbm.at[p, i], schur_v.at[p, :, pl.ds(i * LANES, LANES)]) for i in range(2)]
        for p in range(2)
    ]

    barrier = pltpu.get_barrier_semaphore()

    def greet(where):
        pl.semaphore_signal(barrier, inc=1, device_id=where, device_id_type=MESH)

    for peer in far_first:
        greet({"xy": peer})

    @pl.when(turn > 0)
    def _():
        greet({"gz": turn - 1})

    @pl.when(turn < depth - 1)
    def _():
        greet({"gz": turn + 1})

    def wait_bytes(ref, sem):
        pltpu.make_async_copy(ref, ref, sem).wait()

    def halves_of(ref, p):
        return jnp.concatenate([ref[p, i, h] for h in range(HALVES) for i in range(2)], axis=0)

    def local_part(p):
        iota = lax.broadcasted_iota(jnp.int32, (2 * LANES, 2 * LANES), 0)
        wanted = rows_v[p : p + 1, :]
        for c in range(chips):
            onehot[p, pl.ds(c * 2 * LANES, 2 * LANES), :] = (
                iota + c * 2 * LANES == wanted
            ).astype(F32).astype(BF16)
        for copy in local_loads[p]:
            copy.wait()
        field = halves_of(inner_v, p).astype(BF16)
        solved = combined(dot(field, inverse_v[p, 0]), dot(field, inverse_v[p, 1]))
        solved_v[p] = solved
        rounded = solved.astype(BF16)
        pushed = combined(dot(rounded, coupling_v[p, 0]), dot(rounded, coupling_v[p, 1])).astype(BF16)
        for c in range(chips):
            spread = dot_t(pushed, onehot[p, pl.ds(c * 2 * LANES, 2 * LANES), :]).astype(BF16)
            for h in range(HALVES):
                for q in range(2):
                    parts[p, h, 2 * c + q] = spread[h * ROWS : (h + 1) * ROWS, q * LANES : (q + 1) * LANES]
        for h in range(HALVES):
            landed[p, h, me] = parts[p, h, me]

    def send_parts(p):
        for h in range(HALVES):
            for peer in far_first:
                pltpu.make_async_remote_copy(
                    src_ref=parts.at[p, h, peer],
                    dst_ref=landed.at[p, h, me],
                    send_sem=contrib_send.at[p, h],
                    recv_sem=contrib_sem.at[p, h],
                    device_id={"xy": peer},
                    device_id_type=MESH,
                ).start()

    rows_load.wait()
    inner_load.wait()
    local_part(0)
    pl.semaphore_wait(
        barrier, peers - 1 + jnp.minimum(turn, 1) + jnp.minimum(depth - 1 - turn, 1)
    )
    send_parts(0)
    local_part(1)
    send_parts(1)
    front_load.wait()
    link_load.wait()
    size_load.wait()

    own = me * LANES + lax.broadcasted_iota(jnp.int32, (1, LANES), 1)
    masks = [jnp.where(own < size_ref[p], 1.0, 0.0).astype(F32) for p in range(2)]
    links = [link_v[p : p + 1, :] for p in range(2)]

    def to_next():
        return pltpu.make_async_remote_copy(
            src_ref=mask_out,
            dst_ref=mask_in,
            send_sem=side_send.at[0],
            recv_sem=side_sem.at[0],
            device_id={"gz": turn + 1},
            device_id_type=MESH,
        )

    def to_previous():
        return pltpu.make_async_remote_copy(
            src_ref=ahead,
            dst_ref=ahead_in,
            send_sem=side_send.at[1],
            recv_sem=side_sem.at[1],
            device_id={"gz": turn - 1},
            device_id_type=MESH,
        )

    @pl.when(turn < depth - 1)
    def _():
        mask_out[...] = jnp.broadcast_to(masks[1], mask_out.shape)
        to_next().start()

    def share(g, h, block):
        gathered[g, h, me] = block.astype(BF16)
        for peer in far_first:
            pltpu.make_async_remote_copy(
                src_ref=gathered.at[g, h, me],
                dst_ref=gathered.at[g, h, me],
                send_sem=gather_send.at[g, h],
                recv_sem=gather_sem.at[g, h, chip],
                device_id={"xy": peer},
                device_id_type=MESH,
            ).start()

    near = sum(sum(map(distance, d)) < 2 for d in offsets)
    cross_order = far_first[: 2 * (chips - near)] + [2 * c + core for c in reversed(near_chips[:near])]

    def cross(i, g, h, block, to):
        crossing[i, h] = block.astype(BF16)
        for peer in cross_order:
            pltpu.make_async_remote_copy(
                src_ref=crossing.at[i, h],
                dst_ref=gathered.at[g, h, me],
                send_sem=cross_send.at[i, h],
                recv_sem=gather_sem.at[g, h, chip],
                device_id={"xy": peer, "gz": to},
                device_id_type=MESH,
            ).start()

    def base_of(p, h):
        wait_bytes(landed.at[p, h, pl.ds(0, peers - 1)], contrib_sem.at[p, h])
        total = landed[p, h, 0].astype(F32)
        for i in range(1, peers):
            total = total + landed[p, h, i].astype(F32)
        return jnp.concatenate([front_v[p, i, h] for i in range(2)], axis=0) - total

    for h in range(HALVES):
        base = base_of(0, h)
        masked = masks[0] * base

        @pl.when(turn == 0)
        def _():
            share(FWD0, h, masks[0] * (base + links[0] * jnp.zeros_like(base)))

        @pl.when(turn > 0)
        def _():
            ahead[pl.ds(h * ROWS, ROWS), :] = masked

    @pl.when(turn > 0)
    def _():
        ahead[pl.ds(HALVES * ROWS, 8), :] = jnp.broadcast_to(masks[0] * links[0], (8, LANES))
        to_previous().start()

    for h in range(HALVES):
        base_v[h] = base_of(1, h)
    for p in range(2):
        for copy in schur_loads[p]:
            copy.wait()

    middle = sum(sum(map(distance, d)) < 3 for d in offsets)
    late = list(range(near, middle)) + list(range(near)) + list(range(middle, chips))

    def product(g, h, matrix, arrival, order=None):
        total = None
        for i in order or range(chips):
            c = near_chips[i]
            rows = pl.ds(pl.multiple_of(c * 2 * LANES, 2 * LANES), 2 * LANES)
            held = matrix[rows, :]
            if arrival is not None:
                arrival(g, h, i, c)
            block = jnp.concatenate([gathered[g, h, 2 * c], gathered[g, h, 2 * c + 1]], axis=1)
            term = dot(block, held)
            total = term if total is None else total + term
        return total

    def shared(g, h, i, c):
        wait_bytes(gathered.at[g, h, pl.ds(0, 1 if i == 0 else 2)], gather_sem.at[g, h, c])

    def handed(i, g, h, j):
        slot = 2 * near_chips[j] + core
        return pltpu.make_async_remote_copy(
            src_ref=gathered.at[g, h, slot],
            dst_ref=gathered.at[g, h, slot],
            send_sem=near_send.at[i, h],
            recv_sem=near_sem.at[i, h, j],
            device_id={"xy": 2 * chip + 1 - core},
            device_id_type=MESH,
        )

    def hand_over(i, g, h):
        for j in range(near):
            wait_bytes(gathered.at[g, h, 0], gather_sem.at[g, h, near_chips[j]])
            handed(i, g, h, j).start()

    def crossed(i):
        def wait(g, h, j, c):
            if j < near:
                wait_bytes(gathered.at[g, h, 0], near_sem.at[i, h, j])
            else:
                wait_bytes(gathered.at[g, h, pl.ds(0, 2)], gather_sem.at[g, h, c])

        return wait

    def schur(g, h, p, arrival, order=None):
        out = product(g, h, schur_v.at[p], arrival, order)
        return combined(out[:, :LANES], out[:, LANES:])

    @pl.when(turn == depth - 1)
    def _():
        for h in range(HALVES):
            for i in range(peers):
                gathered[BWD1, h, i] = jnp.zeros((ROWS, LANES), BF16)
            last_v[h] = masks[1] * schur(BWD1, h, 1, None)

    for h in range(HALVES):

        @pl.when(turn == 0)
        def _():
            first_v[h] = masks[0] * schur(FWD0, h, 0, shared)

        @pl.when(turn > 0)
        def _():
            hand_over(0, FWD0, h)
            first_v[h] = masks[0] * schur(FWD0, h, 0, crossed(0), late)

        front = first_v[h]
        share(FWD1, h, masks[1] * (base_v[h] + links[1] * front))

    @pl.when(turn < depth - 1)
    def _():
        pltpu.make_async_copy(ahead_in, ahead_in, side_sem.at[1]).wait()

    for h in range(HALVES):
        front = masks[1] * schur(FWD1, h, 1, shared)

        @pl.when(turn < depth - 1)
        def _():
            cross(
                0,
                FWD0,
                h,
                ahead_in[pl.ds(h * ROWS, ROWS), :] + ahead_in[pl.ds(HALVES * ROWS, 1), :] * front,
                turn + 1,
            )
            last_v[h] = front

        @pl.when(turn == depth - 1)
        def _():
            total = front + last_v[h]
            share(BWD0, h, masks[0] * (links[1] * total))
            last_v[h] = total

    @pl.when(turn < depth - 1)
    def _():
        for h in range(HALVES):
            hand_over(1, BWD1, h)
            total = last_v[h] + masks[1] * schur(BWD1, h, 1, crossed(1), late)
            share(BWD0, h, masks[0] * (links[1] * total))
            last_v[h] = total

    @pl.when(turn == 0)
    def _():
        for h in range(HALVES):
            share(TOT1, h, last_v[h])

    @pl.when(turn > 0)
    def _():
        pltpu.make_async_copy(mask_in, mask_in, side_sem.at[0]).wait()

    for h in range(HALVES):
        total = first_v[h] + masks[0] * schur(BWD0, h, 0, shared)
        first_v[h] = total

        @pl.when(turn > 0)
        def _():
            cross(1, BWD1, h, mask_in[0:1, :] * (links[0] * total), turn - 1)

        @pl.when(turn == 0)
        def _():
            share(TOT0, h, total)

    @pl.when(turn > 0)
    def _():
        for h in range(HALVES):
            share(TOT0, h, first_v[h])
        for h in range(HALVES):
            share(TOT1, h, last_v[h])

    for h in range(HALVES):
        for i in range(2):
            rows = pl.ds(i * (ROWS // 2), ROWS // 2)
            front_res[0, i, h] = first_v[h, rows, :]
            front_res[1, i, h] = last_v[h, rows, :]

    stores = [pltpu.make_async_copy(front_res, front_out, store_sem.at[0])]
    stores[0].start()

    for p, g in ((1, TOT1), (0, TOT0)):
        for h in range(HALVES):
            picked = product(g, h, onehot.at[p], shared).astype(BF16)
            lifted = combined(dot_t(picked, coupling_v[p, 0]), dot_t(picked, coupling_v[p, 1])).astype(BF16)
            inner = solved_v[p, pl.ds(h * ROWS, ROWS), :] - combined(
                dot(lifted, inverse_v[p, 0]), dot(lifted, inverse_v[p, 1])
            )
            for i in range(2):
                inner_res[p, i, h] = inner[i * (ROWS // 2) : (i + 1) * (ROWS // 2)]

        store = pltpu.make_async_copy(inner_res.at[p], inner_out.at[p], store_sem.at[1 + p])
        store.start()
        stores.append(store)

    for h in range(HALVES):
        for p in range(2):
            wait_bytes(parts.at[p, h, pl.ds(0, peers - 1)], contrib_send.at[p, h])
        for g in (FWD1, BWD0, TOT1, TOT0):
            wait_bytes(gathered.at[g, h, pl.ds(0, peers - 1)], gather_send.at[g, h])

    @pl.when(turn == 0)
    def _():
        for h in range(HALVES):
            wait_bytes(gathered.at[FWD0, h, pl.ds(0, peers - 1)], gather_send.at[FWD0, h])

    @pl.when(turn < depth - 1)
    def _():
        for h in range(HALVES):
            wait_bytes(gathered.at[FWD0, h, pl.ds(0, len(cross_order))], cross_send.at[0, h])
            wait_bytes(gathered.at[BWD1, h, pl.ds(0, near)], near_send.at[1, h])
        to_next().wait_send()

    @pl.when(turn > 0)
    def _():
        for h in range(HALVES):
            wait_bytes(gathered.at[BWD1, h, pl.ds(0, len(cross_order))], cross_send.at[1, h])
            wait_bytes(gathered.at[FWD0, h, pl.ds(0, near)], near_send.at[0, h])
        to_previous().wait_send()

    for store in stores:
        store.wait()


def put(inner_in, front_in, inner_out, front_out, inner_v, front_v, sem):
    pairs = ((inner_in, inner_v, inner_out), (front_in, front_v, front_out))
    loads = [pltpu.make_async_copy(src, held, sem.at[0, i]) for i, (src, held, _) in enumerate(pairs)]
    stores = [pltpu.make_async_copy(held, dst, sem.at[1, i]) for i, (_, held, dst) in enumerate(pairs)]
    for copy in loads:
        copy.start()
    for copy, store in zip(loads, stores):
        copy.wait()
        store.start()
    for store in stores:
        store.wait()


def solution(mesh):
    n_xy = mesh.shape["xy"]
    depth = mesh.shape["gz"]
    side = round((n_xy // 2) ** 0.5)

    def on_device(inner, front, inverse, coupling, schur, rows, link, size):
        panels, two, rhs, loc = inner.shape
        unknowns = schur.shape[2]
        bnd = coupling.shape[-1]
        both = two * rhs
        inverse = inverse.reshape(panels, two, loc, loc)
        coupling = coupling.reshape(panels, two, loc, bnd)
        inner = inner.reshape(panels, two, HALVES, rhs // HALVES, loc)
        front = front.reshape(panels, two, HALVES, rhs // HALVES, LANES)
        hbm = pl.BlockSpec(memory_space=pltpu.HBM)
        vmem = pltpu.VMEM
        dma = pltpu.SemaphoreType.DMA
        inner_out, front_out = pl.pallas_call(
            functools.partial(kernel, side, depth),
            out_shape=(
                jax.ShapeDtypeStruct(inner.shape, F32),
                jax.ShapeDtypeStruct(front.shape, F32),
            ),
            in_specs=[hbm] * 8,
            out_specs=(hbm, hbm),
            scratch_shapes=[
                vmem(inner.shape, F32),
                vmem(front.shape, F32),
                vmem(inverse.shape, BF16),
                vmem(coupling.shape, BF16),
                vmem((panels, unknowns, 2 * LANES), BF16),
                vmem(rows.shape, jnp.int32),
                vmem(link.shape, F32),
                pltpu.SMEM(size.shape, jnp.int32),
                vmem((panels, unknowns, bnd), BF16),
                vmem((panels, HALVES, n_xy, ROWS, LANES), BF16),
                vmem((panels, HALVES, n_xy, ROWS, LANES), BF16),
                vmem((6, HALVES, n_xy, ROWS, LANES), BF16),
                vmem((2, HALVES, ROWS, LANES), BF16),
                vmem((HALVES * ROWS + 8, LANES), F32),
                vmem((HALVES * ROWS + 8, LANES), F32),
                vmem((8, LANES), F32),
                vmem((8, LANES), F32),
                vmem((HALVES, ROWS, LANES), F32),
                vmem((HALVES, ROWS, LANES), F32),
                vmem((HALVES, ROWS, LANES), F32),
                vmem((panels, both, loc), F32),
                vmem(inner.shape, F32),
                vmem(front.shape, F32),
                dma((13,)),
                dma((3,)),
                dma((2, HALVES)),
                dma((2, HALVES)),
                dma((6, HALVES)),
                dma((6, HALVES, n_xy // 2)),
                dma((2, HALVES)),
                dma((2, HALVES)),
                dma((2, HALVES, 5)),
                dma((2,)),
                dma((2,)),
            ],
            compiler_params=pltpu.CompilerParams(
                collective_id=0, has_side_effects=True, vmem_limit_bytes=60 << 20
            ),
            name="sweep",
        )(inner, front, inverse, coupling, schur, rows, link, size)
        inner_out, front_out = pl.pallas_call(
            put,
            out_shape=(
                jax.ShapeDtypeStruct(inner.shape, F32),
                jax.ShapeDtypeStruct(front.shape, F32),
            ),
            in_specs=[hbm, hbm],
            out_specs=(hbm, hbm),
            scratch_shapes=[vmem(inner.shape, F32), vmem(front.shape, F32), dma((2, 2))],
            compiler_params=pltpu.CompilerParams(vmem_limit_bytes=60 << 20),
            name="put",
        )(inner_out, front_out)
        return (
            inner_out.reshape(panels, two, rhs, loc),
            front_out.reshape(panels, two, rhs, LANES),
        )

    placed = (
        P("gz", None, None, "xy"),
        P("gz", None, None, "xy"),
        P("gz", "xy", None, None, None),
        P("gz", "xy", None, None, None),
        P("gz", None, None, "xy"),
        P("gz", "xy"),
        P("gz", "xy"),
        P("gz"),
    )
    return jax.shard_map(
        on_device,
        mesh=mesh,
        in_specs=placed,
        out_specs=(P("gz", None, None, "xy"), P("gz", None, None, "xy")),
        check_vma=False,
    )
```

```python
import functools

import jax
import jax.numpy as jnp
from jax import lax
from jax.experimental import pallas as pl
from jax.experimental.pallas import tpu as pltpu
from jax.sharding import PartitionSpec as P

MESH = pl.DeviceIdType.MESH
F32 = jnp.float32
BF16 = jnp.bfloat16
NT = (((1,), (1,)), ((), ()))
LANES = 128

ROWS = 16
HALVES = 2
FWD0, FWD1, BWD1, BWD0, TOT1, TOT0 = range(6)


def dot(a, b):
    return jnp.dot(a, b, preferred_element_type=F32)


def dot_t(a, b):
    return lax.dot_general(a, b, NT, preferred_element_type=F32)


def combined(first, second):
    pieces = []
    for start in range(0, first.shape[0], ROWS):
        mid, end = start + ROWS // 2, start + ROWS
        pieces += [first[start:mid] - second[mid:end], second[start:mid] + first[mid:end]]
    return jnp.concatenate(pieces, axis=0)


def kernel(
    side,
    depth,
    inner_hbm,
    front_hbm,
    inverse_hbm,
    coupling_hbm,
    schur_hbm,
    rows_hbm,
    link_hbm,
    size_hbm,
    inner_out,
    front_out,
    inner_v,
    front_v,
    inverse_v,
    coupling_v,
    schur_v,
    rows_v,
    link_v,
    size_ref,
    onehot,
    parts,
    landed,
    gathered,
    crossing,
    ahead,
    ahead_in,
    mask_out,
    mask_in,
    base_v,
    first_v,
    last_v,
    solved_v,
    inner_res,
    front_res,
    load_sem,
    store_sem,
    contrib_send,
    contrib_sem,
    gather_send,
    gather_sem,
    cross_send,
    near_send,
    near_sem,
    side_send,
    side_sem,
):
    chips = side * side
    peers = 2 * chips
    me = lax.axis_index("xy")
    turn = lax.axis_index("gz")
    core = lax.rem(me, 2)
    chip = me // 2
    chip_x = chip // side
    chip_y = lax.rem(chip, side)

    def chip_at(dx, dy):
        return lax.rem(chip_x + dx, side) * side + lax.rem(chip_y + dy, side)

    def distance(d):
        return min(d, side - d)

    offsets = sorted(
        ((dx, dy) for dx in range(side) for dy in range(side)),
        key=lambda d: (distance(d[0]) + distance(d[1]), d),
    )
    near_chips = [chip_at(*d) for d in offsets]
    far_first = [
        2 * c + lax.rem(core + q, 2) for c in reversed(near_chips[1:]) for q in range(2)
    ] + [2 * chip + 1 - core]

    loads = []

    def load(src, dst):
        copy = pltpu.make_async_copy(src, dst, load_sem.at[len(loads)])
        copy.start()
        loads.append(copy)
        return copy

    rows_load = load(rows_hbm, rows_v)
    inner_load = load(inner_hbm, inner_v)
    local_loads = []
    for p in range(2):
        local_loads.append((load(inverse_hbm.at[p], inverse_v.at[p]), load(coupling_hbm.at[p], coupling_v.at[p])))
    front_load = load(front_hbm, front_v)
    link_load = load(link_hbm, link_v)
    size_load = load(size_hbm, size_ref)
    schur_loads = [
        [load(schur_hbm.at[p, i], schur_v.at[p, :, pl.ds(i * LANES, LANES)]) for i in range(2)]
        for p in range(2)
    ]

    barrier = pltpu.get_barrier_semaphore()

    def greet(where):
        pl.semaphore_signal(barrier, inc=1, device_id=where, device_id_type=MESH)

    for peer in far_first:
        greet({"xy": peer})

    @pl.when(turn > 0)
    def _():
        greet({"gz": turn - 1})

    @pl.when(turn < depth - 1)
    def _():
        greet({"gz": turn + 1})

    def wait_bytes(ref, sem):
        pltpu.make_async_copy(ref, ref, sem).wait()

    def halves_of(ref, p):
        return jnp.concatenate([ref[p, i, h] for h in range(HALVES) for i in range(2)], axis=0)

    def local_part(p):
        iota = lax.broadcasted_iota(jnp.int32, (2 * LANES, 2 * LANES), 0)
        wanted = rows_v[p : p + 1, :]
        for c in range(chips):
            onehot[p, pl.ds(c * 2 * LANES, 2 * LANES), :] = (
                iota + c * 2 * LANES == wanted
            ).astype(F32).astype(BF16)
        for copy in local_loads[p]:
            copy.wait()
        field = halves_of(inner_v, p).astype(BF16)
        solved = combined(dot(field, inverse_v[p, 0]), dot(field, inverse_v[p, 1]))
        solved_v[p] = solved
        rounded = solved.astype(BF16)
        pushed = combined(dot(rounded, coupling_v[p, 0]), dot(rounded, coupling_v[p, 1])).astype(BF16)
        for c in range(chips):
            spread = dot_t(pushed, onehot[p, pl.ds(c * 2 * LANES, 2 * LANES), :]).astype(BF16)
            for h in range(HALVES):
                for q in range(2):
                    parts[p, h, 2 * c + q] = spread[h * ROWS : (h + 1) * ROWS, q * LANES : (q + 1) * LANES]
        for h in range(HALVES):
            landed[p, h, me] = parts[p, h, me]

    def send_parts(p):
        for h in range(HALVES):
            for peer in far_first:
                pltpu.make_async_remote_copy(
                    src_ref=parts.at[p, h, peer],
                    dst_ref=landed.at[p, h, me],
                    send_sem=contrib_send.at[p, h],
                    recv_sem=contrib_sem.at[p, h],
                    device_id={"xy": peer},
                    device_id_type=MESH,
                ).start()

    rows_load.wait()
    inner_load.wait()
    local_part(0)
    pl.semaphore_wait(
        barrier, peers - 1 + jnp.minimum(turn, 1) + jnp.minimum(depth - 1 - turn, 1)
    )
    send_parts(0)
    local_part(1)
    send_parts(1)
    front_load.wait()
    link_load.wait()
    size_load.wait()

    own = me * LANES + lax.broadcasted_iota(jnp.int32, (1, LANES), 1)
    masks = [jnp.where(own < size_ref[p], 1.0, 0.0).astype(F32) for p in range(2)]
    links = [link_v[p : p + 1, :] for p in range(2)]

    def to_next():
        return pltpu.make_async_remote_copy(
            src_ref=mask_out,
            dst_ref=mask_in,
            send_sem=side_send.at[0],
            recv_sem=side_sem.at[0],
            device_id={"gz": turn + 1},
            device_id_type=MESH,
        )

    def to_previous():
        return pltpu.make_async_remote_copy(
            src_ref=ahead,
            dst_ref=ahead_in,
            send_sem=side_send.at[1],
            recv_sem=side_sem.at[1],
            device_id={"gz": turn - 1},
            device_id_type=MESH,
        )

    @pl.when(turn < depth - 1)
    def _():
        mask_out[...] = jnp.broadcast_to(masks[1], mask_out.shape)
        to_next().start()

    def share(g, h, block):
        gathered[g, h, me] = block.astype(BF16)
        for peer in far_first:
            pltpu.make_async_remote_copy(
                src_ref=gathered.at[g, h, me],
                dst_ref=gathered.at[g, h, me],
                send_sem=gather_send.at[g, h],
                recv_sem=gather_sem.at[g, h, chip],
                device_id={"xy": peer},
                device_id_type=MESH,
            ).start()

    near = sum(sum(map(distance, d)) < 2 for d in offsets)
    cross_order = far_first[: 2 * (chips - near)] + [2 * c + core for c in reversed(near_chips[:near])]

    def cross(i, g, h, block, to):
        crossing[i, h] = block.astype(BF16)
        for peer in cross_order:
            pltpu.make_async_remote_copy(
                src_ref=crossing.at[i, h],
                dst_ref=gathered.at[g, h, me],
                send_sem=cross_send.at[i, h],
                recv_sem=gather_sem.at[g, h, chip],
                device_id={"xy": peer, "gz": to},
                device_id_type=MESH,
            ).start()

    def base_of(p, h):
        wait_bytes(landed.at[p, h, pl.ds(0, peers - 1)], contrib_sem.at[p, h])
        total = landed[p, h, 0].astype(F32)
        for i in range(1, peers):
            total = total + landed[p, h, i].astype(F32)
        return jnp.concatenate([front_v[p, i, h] for i in range(2)], axis=0) - total

    for h in range(HALVES):
        base = base_of(0, h)
        masked = masks[0] * base

        @pl.when(turn == 0)
        def _():
            share(FWD0, h, masks[0] * (base + links[0] * jnp.zeros_like(base)))

        @pl.when(turn > 0)
        def _():
            ahead[pl.ds(h * ROWS, ROWS), :] = masked

    @pl.when(turn > 0)
    def _():
        ahead[pl.ds(HALVES * ROWS, 8), :] = jnp.broadcast_to(masks[0] * links[0], (8, LANES))
        to_previous().start()

    for h in range(HALVES):
        base_v[h] = base_of(1, h)
    for p in range(2):
        for copy in schur_loads[p]:
            copy.wait()

    middle = sum(sum(map(distance, d)) < 3 for d in offsets)
    late = list(range(near, middle)) + list(range(near)) + list(range(middle, chips))

    def product(g, h, matrix, arrival, order=None):
        total = None
        for i in order or range(chips):
            c = near_chips[i]
            rows = pl.ds(pl.multiple_of(c * 2 * LANES, 2 * LANES), 2 * LANES)
            held = matrix[rows, :]
            if arrival is not None:
                arrival(g, h, i, c)
            block = jnp.concatenate([gathered[g, h, 2 * c], gathered[g, h, 2 * c + 1]], axis=1)
            term = dot(block, held)
            total = term if total is None else total + term
        return total

    def shared(g, h, i, c):
        wait_bytes(gathered.at[g, h, pl.ds(0, 1 if i == 0 else 2)], gather_sem.at[g, h, c])

    def handed(i, g, h, j):
        slot = 2 * near_chips[j] + core
        return pltpu.make_async_remote_copy(
            src_ref=gathered.at[g, h, slot],
            dst_ref=gathered.at[g, h, slot],
            send_sem=near_send.at[i, h],
            recv_sem=near_sem.at[i, h, j],
            device_id={"xy": 2 * chip + 1 - core},
            device_id_type=MESH,
        )

    def hand_over(i, g, h):
        for j in range(near):
            wait_bytes(gathered.at[g, h, 0], gather_sem.at[g, h, near_chips[j]])
            handed(i, g, h, j).start()

    def crossed(i):
        def wait(g, h, j, c):
            if j < near:
                wait_bytes(gathered.at[g, h, 0], near_sem.at[i, h, j])
            else:
                wait_bytes(gathered.at[g, h, pl.ds(0, 2)], gather_sem.at[g, h, c])

        return wait

    def schur(g, h, p, arrival, order=None):
        out = product(g, h, schur_v.at[p], arrival, order)
        return combined(out[:, :LANES], out[:, LANES:])

    @pl.when(turn == depth - 1)
    def _():
        for h in range(HALVES):
            for i in range(peers):
                gathered[BWD1, h, i] = jnp.zeros((ROWS, LANES), BF16)
            last_v[h] = masks[1] * schur(BWD1, h, 1, None)

    for h in range(HALVES):

        @pl.when(turn == 0)
        def _():
            first_v[h] = masks[0] * schur(FWD0, h, 0, shared)

        @pl.when(turn > 0)
        def _():
            hand_over(0, FWD0, h)
            first_v[h] = masks[0] * schur(FWD0, h, 0, crossed(0), late)

        front = first_v[h]
        share(FWD1, h, masks[1] * (base_v[h] + links[1] * front))

    @pl.when(turn < depth - 1)
    def _():
        pltpu.make_async_copy(ahead_in, ahead_in, side_sem.at[1]).wait()

    for h in range(HALVES):
        front = masks[1] * schur(FWD1, h, 1, shared)

        @pl.when(turn < depth - 1)
        def _():
            cross(
                0,
                FWD0,
                h,
                ahead_in[pl.ds(h * ROWS, ROWS), :] + ahead_in[pl.ds(HALVES * ROWS, 1), :] * front,
                turn + 1,
            )
            last_v[h] = front

        @pl.when(turn == depth - 1)
        def _():
            total = front + last_v[h]
            share(BWD0, h, masks[0] * (links[1] * total))
            last_v[h] = total

    @pl.when(turn < depth - 1)
    def _():
        for h in range(HALVES):
            hand_over(1, BWD1, h)
            total = last_v[h] + masks[1] * schur(BWD1, h, 1, crossed(1), late)
            share(BWD0, h, masks[0] * (links[1] * total))
            last_v[h] = total

            @pl.when(turn == 0)
            def _():
                share(TOT1, h, total)

    @pl.when(turn > 0)
    def _():
        pltpu.make_async_copy(mask_in, mask_in, side_sem.at[0]).wait()

    for h in range(HALVES):
        total = first_v[h] + masks[0] * schur(BWD0, h, 0, shared)
        first_v[h] = total

        @pl.when(turn > 0)
        def _():
            cross(1, BWD1, h, mask_in[0:1, :] * (links[0] * total), turn - 1)

        @pl.when(turn == 0)
        def _():
            share(TOT0, h, total)

    @pl.when(turn > 0)
    def _():
        for h in range(HALVES):
            share(TOT0, h, first_v[h])
        for h in range(HALVES):
            share(TOT1, h, last_v[h])

    for h in range(HALVES):
        for i in range(2):
            rows = pl.ds(i * (ROWS // 2), ROWS // 2)
            front_res[0, i, h] = first_v[h, rows, :]
            front_res[1, i, h] = last_v[h, rows, :]

    stores = [pltpu.make_async_copy(front_res, front_out, store_sem.at[0])]
    stores[0].start()

    for p, g in ((1, TOT1), (0, TOT0)):
        for h in range(HALVES):
            picked = product(g, h, onehot.at[p], shared).astype(BF16)
            lifted = combined(dot_t(picked, coupling_v[p, 0]), dot_t(picked, coupling_v[p, 1])).astype(BF16)
            inner = solved_v[p, pl.ds(h * ROWS, ROWS), :] - combined(
                dot(lifted, inverse_v[p, 0]), dot(lifted, inverse_v[p, 1])
            )
            for i in range(2):
                inner_res[p, i, h] = inner[i * (ROWS // 2) : (i + 1) * (ROWS // 2)]

        store = pltpu.make_async_copy(inner_res.at[p], inner_out.at[p], store_sem.at[1 + p])
        store.start()
        stores.append(store)

    for h in range(HALVES):
        for p in range(2):
            wait_bytes(parts.at[p, h, pl.ds(0, peers - 1)], contrib_send.at[p, h])
        for g in (FWD1, BWD0, TOT1, TOT0):
            wait_bytes(gathered.at[g, h, pl.ds(0, peers - 1)], gather_send.at[g, h])

    @pl.when(turn == 0)
    def _():
        for h in range(HALVES):
            wait_bytes(gathered.at[FWD0, h, pl.ds(0, peers - 1)], gather_send.at[FWD0, h])

    @pl.when(turn < depth - 1)
    def _():
        for h in range(HALVES):
            wait_bytes(gathered.at[FWD0, h, pl.ds(0, len(cross_order))], cross_send.at[0, h])
            wait_bytes(gathered.at[BWD1, h, pl.ds(0, near)], near_send.at[1, h])
        to_next().wait_send()

    @pl.when(turn > 0)
    def _():
        for h in range(HALVES):
            wait_bytes(gathered.at[BWD1, h, pl.ds(0, len(cross_order))], cross_send.at[1, h])
            wait_bytes(gathered.at[FWD0, h, pl.ds(0, near)], near_send.at[0, h])
        to_previous().wait_send()

    for store in stores:
        store.wait()


def put(inner_in, front_in, inner_out, front_out, inner_v, front_v, sem):
    pairs = ((inner_in, inner_v, inner_out), (front_in, front_v, front_out))
    loads = [pltpu.make_async_copy(src, held, sem.at[0, i]) for i, (src, held, _) in enumerate(pairs)]
    stores = [pltpu.make_async_copy(held, dst, sem.at[1, i]) for i, (_, held, dst) in enumerate(pairs)]
    for copy in loads:
        copy.start()
    for copy, store in zip(loads, stores):
        copy.wait()
        store.start()
    for store in stores:
        store.wait()


def solution(mesh):
    n_xy = mesh.shape["xy"]
    depth = mesh.shape["gz"]
    side = round((n_xy // 2) ** 0.5)

    def on_device(inner, front, inverse, coupling, schur, rows, link, size):
        panels, two, rhs, loc = inner.shape
        unknowns = schur.shape[2]
        bnd = coupling.shape[-1]
        both = two * rhs
        inverse = inverse.reshape(panels, two, loc, loc)
        coupling = coupling.reshape(panels, two, loc, bnd)
        inner = inner.reshape(panels, two, HALVES, rhs // HALVES, loc)
        front = front.reshape(panels, two, HALVES, rhs // HALVES, LANES)
        hbm = pl.BlockSpec(memory_space=pltpu.HBM)
        vmem = pltpu.VMEM
        dma = pltpu.SemaphoreType.DMA
        inner_out, front_out = pl.pallas_call(
            functools.partial(kernel, side, depth),
            out_shape=(
                jax.ShapeDtypeStruct(inner.shape, F32),
                jax.ShapeDtypeStruct(front.shape, F32),
            ),
            in_specs=[hbm] * 8,
            out_specs=(hbm, hbm),
            scratch_shapes=[
                vmem(inner.shape, F32),
                vmem(front.shape, F32),
                vmem(inverse.shape, BF16),
                vmem(coupling.shape, BF16),
                vmem((panels, unknowns, 2 * LANES), BF16),
                vmem(rows.shape, jnp.int32),
                vmem(link.shape, F32),
                pltpu.SMEM(size.shape, jnp.int32),
                vmem((panels, unknowns, bnd), BF16),
                vmem((panels, HALVES, n_xy, ROWS, LANES), BF16),
                vmem((panels, HALVES, n_xy, ROWS, LANES), BF16),
                vmem((6, HALVES, n_xy, ROWS, LANES), BF16),
                vmem((2, HALVES, ROWS, LANES), BF16),
                vmem((HALVES * ROWS + 8, LANES), F32),
                vmem((HALVES * ROWS + 8, LANES), F32),
                vmem((8, LANES), F32),
                vmem((8, LANES), F32),
                vmem((HALVES, ROWS, LANES), F32),
                vmem((HALVES, ROWS, LANES), F32),
                vmem((HALVES, ROWS, LANES), F32),
                vmem((panels, both, loc), F32),
                vmem(inner.shape, F32),
                vmem(front.shape, F32),
                dma((13,)),
                dma((3,)),
                dma((2, HALVES)),
                dma((2, HALVES)),
                dma((6, HALVES)),
                dma((6, HALVES, n_xy // 2)),
                dma((2, HALVES)),
                dma((2, HALVES)),
                dma((2, HALVES, 5)),
                dma((2,)),
                dma((2,)),
            ],
            compiler_params=pltpu.CompilerParams(
                collective_id=0, has_side_effects=True, vmem_limit_bytes=60 << 20
            ),
            name="sweep",
        )(inner, front, inverse, coupling, schur, rows, link, size)
        inner_out, front_out = pl.pallas_call(
            put,
            out_shape=(
                jax.ShapeDtypeStruct(inner.shape, F32),
                jax.ShapeDtypeStruct(front.shape, F32),
            ),
            in_specs=[hbm, hbm],
            out_specs=(hbm, hbm),
            scratch_shapes=[vmem(inner.shape, F32), vmem(front.shape, F32), dma((2, 2))],
            compiler_params=pltpu.CompilerParams(vmem_limit_bytes=60 << 20),
            name="put",
        )(inner_out, front_out)
        return (
            inner_out.reshape(panels, two, rhs, loc),
            front_out.reshape(panels, two, rhs, LANES),
        )

    placed = (
        P("gz", None, None, "xy"),
        P("gz", None, None, "xy"),
        P("gz", "xy", None, None, None),
        P("gz", "xy", None, None, None),
        P("gz", None, None, "xy"),
        P("gz", "xy"),
        P("gz", "xy"),
        P("gz"),
    )
    return jax.shard_map(
        on_device,
        mesh=mesh,
        in_specs=placed,
        out_specs=(P("gz", None, None, "xy"), P("gz", None, None, "xy")),
        check_vma=False,
    )
```
